32 devices in a mesh: grp: 2 (over x), pool: 16 (over z, y, core).
Axes of the slice: x: 2, y: 2, z: 4, core: 2. Of those that a mesh axis runs over, the one named last changes fastest.
Arguments:
- queries: bfloat16 [32, 128, 1024], P(('grp', 'pool')), parts along dimension 0, may hold values from -400 to 400
- new_kv: bfloat16 [32, 128, 256], P(('grp', 'pool')), parts along dimension 0, may hold values from -16 to 16
- pool_kv: bfloat16 [64, 8, 128, 256], P(('grp', 'pool')), parts along dimension 0, may hold values from -16 to 16
- hit_slots: int32 [4, 16], P('grp'), parts along dimension 0, may hold values from 0 to 31, as said below
- prefix_blocks: int32 [4], P('grp'), parts along dimension 0, may hold values from 1 to 16, 20 in all
- new_owners: int32 [4, 2], P('grp'), parts along dimension 0, may hold values from 0 to 15, as said below
Outputs:
- attended: bfloat16 [32, 128, 1024], P(('grp', 'pool')), parts along dimension 0
- new_store: bfloat16 [32, 8, 128, 256], P(('grp', 'pool')), parts along dimension 0
The draws below stay inside these ranges and needn't reach their ends.
There are 2 independent parts, one for each index of `grp`. The reference program is written for one: setup_inputs(seed, part) draws one part's arguments, and reference() takes and returns one part's arrays. A program takes and returns all parts, laid end to end along the dimension named above; each array names one. Nothing has to cross between parts.
Inputs may be any that keep to these rules, and one draw needn't show every extreme that they name: `hit_slots`: slot s lies on owner s // 2. Block j of request r lies on owner (f + j) mod 16, where f depends on r and is a multiple of 4; one owner keeps different requests in different slots. Entries with j >= prefix_blocks[r] are unused. `prefix_blocks`: they sum to 20. `new_owners`: all 4 entries are distinct.
All inputs are finite; a program needn't handle non-finite values.
Results may differ from the reference program's by a relative error of at most 0.009.
Values may be sent and summed in bfloat16 or wider, within the bound.
No kernel may reach another device: no remote copies, remote signals or barrier semaphores. Data moves between devices by JAX's collectives and lax.ppermute only.
A program may use at most 64 MiB of HBM per device.

```python
import math
import jax
import jax.numpy as jnp
import numpy as np
from jax import lax

HD = 128
KVH = 8
G = 8
BLK = 128
OWNERS = 16
REQS = 2
SLOTS = 2
MAXB = 16


def suffix_parts(key):
    base = jax.random.fold_in(key, 7)
    key_a, key_b, key_c = jax.random.split(base, 3)
    key_rows = jax.random.truncated_normal(key_a, -4.0, 4.0, (REQS * KVH, BLK, HD), jnp.float32)
    value_rows = 4.0 * jax.random.truncated_normal(key_b, -4.0, 4.0, (REQS * KVH, BLK, HD), jnp.float32)
    query_rows = 1.5 * jax.random.truncated_normal(key_c, -4.0, 4.0, (REQS * KVH, BLK, G, HD), jnp.float32)
    return (query_rows, key_rows, value_rows)


def draw_queries(key, part):
    query_rows, key_rows, value_rows = suffix_parts(key)
    return query_rows.reshape(REQS * KVH, BLK, G * HD).astype(jnp.bfloat16)


def draw_new_kv(key, part):
    query_rows, key_rows, value_rows = suffix_parts(key)
    return jnp.concatenate([key_rows, value_rows], 2).astype(jnp.bfloat16)


def draw_pool_kv(key, part):
    base = jax.random.fold_in(key, 13)
    shape = (OWNERS * SLOTS, KVH, BLK, 2 * HD)
    scales = jnp.concatenate([jnp.ones((HD,), jnp.float32), 4.0 * jnp.ones((HD,), jnp.float32)])
    raw = jax.random.truncated_normal(base, -4.0, 4.0, shape, jnp.float32)
    return (raw * scales).astype(jnp.bfloat16)


def draw_hit_slots(key, part):
    base = jax.random.fold_in(key, 17)
    key_a, key_b = jax.random.split(base)
    first_owner = 4 * jax.random.randint(key_a, (REQS,), 0, MAXB // 4)
    owner = (first_owner[:, None] + jnp.arange(MAXB)[None, :]) % MAXB
    orders = jax.vmap(lambda sub_key: jax.random.permutation(sub_key, SLOTS))(jax.random.split(key_b, MAXB))
    local_slot = orders[owner, jnp.arange(REQS)[:, None]]
    return (owner * SLOTS + local_slot).astype(jnp.int32)


def draw_new_owners(key, part):
    base = jax.random.fold_in(key, 19)
    chosen = jax.random.permutation(base, OWNERS)[:2 * REQS]
    return chosen.reshape(REQS, 2).astype(jnp.int32)


def profile(number_of, total, most, lean):
    portions = [(1 << 20) // math.isqrt(rank ** lean) + 1 for rank in range(2, number_of + 1)]
    spare, counts = total - most - (number_of - 1), [1] * (number_of - 1)
    while spare > 0:
        candidates = [i for i in range(number_of - 1) if counts[i] < most]
        mass, budget = sum([portions[i] for i in candidates]), spare
        for i in candidates:
            more = min(most - counts[i], max(1, budget * portions[i] // mass), spare)
            counts[i] = counts[i] + more
            spare = spare - more
    return np.array([most] + counts)


def uneven_parts(rng, amount, total, limit, slope):
    if amount == 2:
        one = jax.random.randint(rng, (), max(1, total - limit), min(limit, total - 1) + 1)
        return jnp.stack([one, total - one])
    lengths = jnp.asarray(profile(amount, total, limit, slope), jnp.int32)
    pairs = (amount - 1) // 2
    donor, taker = lengths[1:1 + 2 * pairs:2], lengths[2:2 + 2 * pairs:2]
    room = jnp.minimum(donor - 1, limit - taker)
    moved = jax.random.randint(jax.random.fold_in(rng, 1), (pairs,), 0, 1 << 20) % (room + 1)
    lengths = lengths.at[1:1 + 2 * pairs:2].set(donor - moved).at[2:2 + 2 * pairs:2].set(taker + moved)
    return lengths[jax.random.permutation(jax.random.fold_in(rng, 2), amount)]


def setup_inputs(seed: int = 0, part: int = 0) -> dict:
    seeds = jax.random.split(jax.random.key(seed), 7)
    part_splits = jax.random.split(jax.random.fold_in(seeds[6], part), 7)
    return {
        "queries": draw_queries(jax.random.fold_in(jax.random.fold_in(seeds[6], part), 71), part),
        "new_kv": draw_new_kv(jax.random.fold_in(jax.random.fold_in(seeds[6], part), 71), part),
        "pool_kv": draw_pool_kv(jax.random.fold_in(jax.random.fold_in(seeds[6], part), 71), part),
        "hit_slots": draw_hit_slots(jax.random.fold_in(jax.random.fold_in(seeds[6], part), 71), part),
        "prefix_blocks": uneven_parts(part_splits[4], REQS, 5 * REQS * MAXB // 8, MAXB, 2).astype(jnp.int32),
        "new_owners": draw_new_owners(jax.random.fold_in(jax.random.fold_in(seeds[6], part), 71), part),
    }


def reference(queries, new_kv, pool_kv, hit_slots, prefix_blocks, new_owners):
    score_scale = 1.0 / (HD ** 0.5)
    prefix_len = MAXB * BLK
    causal = jnp.arange(BLK)[None, :] <= jnp.arange(BLK)[:, None]

    def one_pair(pair_index):
        request = pair_index // KVH
        head = pair_index % KVH
        slots_used = hit_slots[request]
        cached = pool_kv[slots_used, head].reshape(prefix_len, 2 * HD)
        fresh = new_kv[pair_index]
        key_rows = jnp.concatenate([cached[:, :HD], fresh[:, :HD]], 0).astype(jnp.float32)
        value_rows = jnp.concatenate([cached[:, HD:], fresh[:, HD:]], 0).astype(jnp.float32)
        query_rows = queries[pair_index].reshape(BLK, G, HD).astype(jnp.float32)
        scores = jnp.einsum("tgd,kd->tgk", query_rows, key_rows) * score_scale
        in_prefix = jnp.arange(prefix_len) < prefix_blocks[request] * BLK
        usable = jnp.concatenate([jnp.broadcast_to(in_prefix[None, :], (BLK, prefix_len)), causal], 1)[:, None, :]
        scores = jnp.where(usable, scores, -jnp.inf)
        row_max = jnp.max(scores, axis=2, keepdims=True)
        weights = jnp.exp(scores - row_max)
        totals = jnp.sum(weights, axis=2)
        rounded = lax.optimization_barrier(weights.astype(jnp.bfloat16)).astype(jnp.float32)
        mixed = jnp.einsum("tgk,kd->tgd", rounded, value_rows) / totals[:, :, None]
        return mixed.reshape(BLK, G * HD).astype(jnp.bfloat16)

    attended = lax.map(one_pair, jnp.arange(REQS * KVH, dtype=jnp.int32))
    grouped = new_kv.reshape(REQS, KVH, BLK, 2 * HD)
    new_store = jnp.zeros((OWNERS, KVH, BLK, 2 * HD), jnp.bfloat16)
    new_store = new_store.at[new_owners[:, 0]].set(grouped).at[new_owners[:, 1]].set(grouped)
    return attended, new_store
```

```python
import functools
import math

import jax
import jax.numpy as jnp
from jax import lax
from jax.experimental import pallas as pl
from jax.experimental.pallas import tpu as pltpu
from jax.sharding import PartitionSpec as P

MINUS_BIG = -1e30
ANY = pl.BlockSpec(memory_space=pl.ANY)
SMEM = pl.BlockSpec(memory_space=pltpu.SMEM)


def owner_position(hits_ref, request, owner, slots, pool):
    first = hits_ref[request, 0] // slots
    return lax.rem(owner - first + pool, pool)


def held_slot(hits_ref, blocks_ref, request, me, slots, pool):
    position = owner_position(hits_ref, request, me, slots, pool)
    longest = hits_ref.shape[1]
    entry = hits_ref[request, jnp.minimum(position, longest - 1)]
    return jnp.where(position < blocks_ref[request], lax.rem(entry, slots), 0)


def wanted_request(owners_ref, device):
    found = jnp.int32(0)
    any_found = jnp.bool_(False)
    for request in range(owners_ref.shape[0]):
        for copy in range(owners_ref.shape[1]):
            hit = owners_ref[request, copy] == device
            found = jnp.where(hit, request, found)
            any_found = jnp.logical_or(any_found, hit)
    return found, any_found


def pack_far_kernel(plan, sizes, hits_ref, blocks_ref, pool_ref, *rest):
    slots, heads, pool = sizes
    outs, (stage, in_sems, out_sems) = rest[: len(plan)], rest[len(plan) :]
    me = lax.axis_index("pool")
    loads = []
    row = 0
    for index, targets in enumerate(plan):
        for place, k in enumerate(targets):
            other = lax.bitwise_xor(me, k)
            request = other // heads
            slot = held_slot(hits_ref, blocks_ref, request, me, slots, pool)
            load = pltpu.make_async_copy(
                pool_ref.at[slot, lax.rem(other, heads)], stage.at[row], in_sems.at[row]
            )
            load.start()
            loads.append((load, row, index, place))
            row += 1
    stores = []
    for load, row, index, place in loads:
        load.wait()
        store = pltpu.make_async_copy(stage.at[row], outs[index].at[place], out_sems.at[row])
        store.start()
        stores.append(store)
    for store in stores:
        store.wait()


def pack_far(plan, hits, blocks, pool_kv, pool):
    slots, heads, length, width = pool_kv.shape
    rows = sum(len(targets) for targets in plan)
    return pl.pallas_call(
        functools.partial(pack_far_kernel, plan, (slots, heads, pool)),
        out_shape=[
            jax.ShapeDtypeStruct((len(targets), length, width), pool_kv.dtype) for targets in plan
        ],
        in_specs=[SMEM, SMEM, ANY],
        out_specs=[ANY] * len(plan),
        scratch_shapes=[
            pltpu.VMEM((rows, length, width), pool_kv.dtype),
            pltpu.SemaphoreType.DMA((rows,)),
            pltpu.SemaphoreType.DMA((rows,)),
        ],
        name="pack_far",
    )(hits, blocks, pool_kv)


def pack_near_kernel(near, sizes, hits_ref, blocks_ref, owners_ref, pool_ref, *rest):
    slots, heads, pool, requests = sizes
    news, rest = rest[:requests], rest[requests:]
    outs, (stage, fresh, in_sems, fresh_sems, out_sems) = rest[: len(near)], rest[len(near) :]
    me = lax.axis_index("pool")
    mine = me // heads
    fresh_loads = []
    for m in range(requests):
        load = pltpu.make_async_copy(news[m].at[0], fresh.at[m], fresh_sems.at[m])
        load.start()
        fresh_loads.append(load)
    slot = held_slot(hits_ref, blocks_ref, mine, me, slots, pool)
    loads = []
    for index, k in enumerate(near):
        other = lax.bitwise_xor(me, k)
        load = pltpu.make_async_copy(
            pool_ref.at[slot, lax.rem(other, heads)], stage.at[index], in_sems.at[index]
        )
        load.start()
        loads.append(load)
    for load in fresh_loads:
        load.wait()
    stores = []
    for index, k in enumerate(near):
        wanted, _ = wanted_request(owners_ref, lax.bitwise_xor(me, k))
        store = pltpu.make_async_copy(
            fresh.at[lax.bitwise_xor(wanted, mine)], outs[index].at[1], out_sems.at[2 * index]
        )
        store.start()
        stores.append(store)
    for index, k in enumerate(near):
        loads[index].wait()
        store = pltpu.make_async_copy(
            stage.at[index], outs[index].at[0], out_sems.at[2 * index + 1]
        )
        store.start()
        stores.append(store)
    for store in stores:
        store.wait()


def pack_near(near, hits, blocks, owners, pool_kv, news, pool):
    slots, heads, length, width = pool_kv.shape
    count = len(near)
    return pl.pallas_call(
        functools.partial(pack_near_kernel, near, (slots, heads, pool, len(news))),
        out_shape=[jax.ShapeDtypeStruct((2, length, width), pool_kv.dtype)] * count,
        in_specs=[SMEM, SMEM, SMEM, ANY] + [ANY] * len(news),
        out_specs=[ANY] * count,
        scratch_shapes=[
            pltpu.VMEM((count, length, width), pool_kv.dtype),
            pltpu.VMEM((len(news), length, width), pool_kv.dtype),
            pltpu.SemaphoreType.DMA((count,)),
            pltpu.SemaphoreType.DMA((len(news),)),
            pltpu.SemaphoreType.DMA((2 * count,)),
        ],
        name="pack_near",
    )(hits, blocks, owners, pool_kv, *news)


def store_new_kernel(near, sizes, owners_ref, *rest):
    heads, requests = sizes
    news, rest = rest[:requests], rest[requests:]
    pieces, rest = rest[: len(near)], rest[len(near) :]
    out_ref, stage, in_sems, out_sems = rest
    me = lax.axis_index("pool")
    mine = me // heads
    head = lax.rem(me, heads)
    wanted, owned = wanted_request(owners_ref, me)

    @pl.when(owned)
    def _():
        for m in range(requests):
            @pl.when(lax.bitwise_xor(wanted, mine) == m)
            def _(m=m):
                pltpu.make_async_copy(news[m].at[0], stage.at[0], in_sems.at[0]).start()
        for index, _k in enumerate(near):
            load = pltpu.make_async_copy(
                pieces[index].at[1], stage.at[1 + index], in_sems.at[1 + index]
            )
            load.start()
        for index in range(len(near) + 1):
            pltpu.make_async_copy(news[0].at[0], stage.at[index], in_sems.at[index]).wait()

    @pl.when(jnp.logical_not(owned))
    def _():
        stage[...] = jnp.zeros_like(stage)

    stores = []
    for index, k in enumerate((0,) + tuple(near)):
        store = pltpu.make_async_copy(
            stage.at[index], out_ref.at[0, lax.bitwise_xor(head, k)], out_sems.at[index]
        )
        store.start()
        stores.append(store)
    for store in stores:
        store.wait()


def store_new(near, owners, news, pieces, heads):
    _, length, width = news[0].shape
    count = len(near) + 1
    return pl.pallas_call(
        functools.partial(store_new_kernel, near, (heads, len(news))),
        out_shape=jax.ShapeDtypeStruct((1, heads, length, width), news[0].dtype),
        in_specs=[SMEM] + [ANY] * (len(news) + len(pieces)),
        out_specs=ANY,
        scratch_shapes=[
            pltpu.VMEM((count, length, width), news[0].dtype),
            pltpu.SemaphoreType.DMA((count,)),
            pltpu.SemaphoreType.DMA((count,)),
        ],
        name="store_new",
    )(owners, *news, *pieces)


def attend_kernel(keys, sizes, first, last, hits_ref, blocks_ref, query_ref, *rest):
    slots, heads, pool, arrays = sizes
    kv_refs, rest = rest[:arrays], rest[arrays:]
    if not first:
        (acc_in, stat_in), rest = rest[:2], rest[2:]
    if last:
        (out_ref,), rest = rest[:1], rest[1:]
    else:
        (acc_out, stat_out), rest = rest[:2], rest[2:]
    kv, kv_sems = rest
    me = lax.axis_index("pool")
    request = me // heads
    length = query_ref.shape[1]
    width = kv.shape[1]
    head_dim = width // 2
    groups = query_ref.shape[2] // head_dim
    loads = []
    for index, (_k, array, place) in enumerate(keys):
        load = pltpu.make_async_copy(
            kv_refs[array].at[place], kv.at[pl.ds(index * length, length)], kv_sems.at[index]
        )
        load.start()
        loads.append(load)
    alive = []
    for k, _array, _place in keys:
        if k is None:
            alive.append(None)
        else:
            position = owner_position(hits_ref, request, lax.bitwise_xor(me, k), slots, pool)
            alive.append(position < blocks_ref[request])
    for load in loads:
        load.wait()
    to_exponent = math.log2(math.e) / math.sqrt(head_dim)
    causal = lax.broadcasted_iota(jnp.int32, (length, length), 1) <= lax.broadcasted_iota(
        jnp.int32, (length, length), 0
    )
    for group in range(groups):
        rows = slice(group * length, (group + 1) * length)
        query = query_ref[0, :, group * head_dim : (group + 1) * head_dim]
        scores = lax.dot_general(
            query,
            kv[:, :head_dim],
            (((1,), (1,)), ((), ())),
            preferred_element_type=jnp.float32,
        )
        parts = []
        for index, live in enumerate(alive):
            part = scores[:, index * length : (index + 1) * length]
            parts.append(jnp.where(causal if live is None else live, part, MINUS_BIG))
        scores = jnp.concatenate(parts, 1)
        top = jnp.max(scores, axis=1, keepdims=True)
        if not first:
            old = stat_in[rows, :]
            old_top = old[:, :1]
            old_total = old[:, head_dim // 2 : head_dim // 2 + 1]
            top = jnp.maximum(top, old_top)
            factor = jnp.exp2((old_top - top) * to_exponent)
        weights = jnp.exp2((scores - top) * to_exponent)
        total = jnp.sum(weights, axis=1, keepdims=True)
        mixed = lax.dot_general(
            weights.astype(jnp.bfloat16),
            kv[:, head_dim:],
            (((1,), (0,)), ((), ())),
            preferred_element_type=jnp.float32,
        )
        if not first:
            total = total + old_total * factor
            mixed = mixed + acc_in[rows, :] * factor
        if last:
            out_ref[0, :, group * head_dim : (group + 1) * head_dim] = (mixed / total).astype(
                out_ref.dtype
            )
        else:
            acc_out[rows, :] = mixed
            lane = lax.broadcasted_iota(jnp.int32, (length, head_dim), 1)
            stat_out[rows, :] = jnp.where(lane < head_dim // 2, top, total)


def attend(keys, hits, blocks, queries, arrays, state, last, slots, heads, pool):
    _, length, columns = queries.shape
    width = arrays[0].shape[-1]
    head_dim = width // 2
    rows = columns // head_dim * length
    first = state is None
    whole = pl.BlockSpec(memory_space=pltpu.VMEM)
    state_shape = jax.ShapeDtypeStruct((rows, head_dim), jnp.float32)
    scores = rows * len(keys) * length
    return pl.pallas_call(
        functools.partial(attend_kernel, keys, (slots, heads, pool, len(arrays)), first, last),
        out_shape=jax.ShapeDtypeStruct(queries.shape, queries.dtype)
        if last
        else (state_shape, state_shape),
        in_specs=[SMEM, SMEM, whole] + [ANY] * len(arrays) + ([] if first else [whole] * 2),
        out_specs=whole if last else (whole, whole),
        scratch_shapes=[
            pltpu.VMEM((len(keys) * length, width), jnp.bfloat16),
            pltpu.SemaphoreType.DMA((len(keys),)),
        ],
        cost_estimate=pl.CostEstimate(
            flops=4 * scores * head_dim,
            bytes_accessed=4 * rows * width,
            transcendentals=scores,
        ),
    )(hits, blocks, queries, *arrays, *(() if first else state))


def on_device(sizes, queries, new_kv, pool_kv, hits, blocks, owners):
    pool, far_pairs, far_last, near = sizes
    slots, heads, _, _ = pool_kv.shape
    requests = hits.shape[0]

    def swap(k, array):
        return lax.ppermute(array, "pool", [(p, p ^ k) for p in range(pool)])

    news = [new_kv] + [swap(m * heads, new_kv) for m in range(1, requests)]
    plan = [(k, k ^ 1) for k in far_pairs] + [(k,) for k in far_last]
    *packed, own = pack_far([*plan, (0,)], hits, blocks, pool_kv, pool)
    far = [swap(k[0], array) for k, array in zip(plan, packed)]
    near_packed = pack_near(near, hits, blocks, owners, pool_kv, news, pool)
    pieces = [swap(k, array) for k, array in zip(near, near_packed)]
    mates = [swap(1, array) for k, array in zip(plan, far) if len(k) == 2]
    common = dict(slots=slots, heads=heads, pool=pool)
    keys = [(None, 0, 0), (0, 1, 0)] + [(k, 2 + i, 0) for i, k in enumerate(near)]
    state = attend(
        keys, hits, blocks, queries, [new_kv, own, *pieces], None, False,
        **common,
    )
    new_store = store_new(near, owners, news, pieces, heads)
    count = len(far_pairs)
    keys = [(k, i, 0) for i, k in enumerate(far_pairs)]
    keys += [(k ^ 1, count + i, 1) for i, k in enumerate(far_pairs)]
    state = attend(
        keys, hits, blocks, queries, [*far[:count], *mates], state, False,
        **common,
    )
    keys = [(k, i, 0) for i, k in enumerate(far_last)]
    attended = attend(
        keys, hits, blocks, queries, far[count:], state, True,
        **common,
    )
    return attended, new_store


def solution(mesh):
    pool = mesh.shape["pool"]
    placed = (
        P(("grp", "pool"), None, None),
        P(("grp", "pool"), None, None),
        P(("grp", "pool"), None, None, None),
        P("grp", None),
        P("grp"),
        P("grp", None),
    )

    def whole(queries, new_kv, pool_kv, hits, blocks, owners):
        heads = pool_kv.shape[1]
        far_all = list(range(heads, pool, 2))
        far_all = far_all[len(far_all) // 2 :] + far_all[: len(far_all) // 2]
        far_pairs, final = far_all[:-1], far_all[-1]
        far_last = [final, final ^ 1]
        near = tuple(range(1, heads))
        sizes = (pool, far_pairs, far_last, near)
        step = jax.shard_map(
            functools.partial(on_device, sizes),
            mesh=mesh,
            in_specs=placed,
            out_specs=(P(("grp", "pool"), None, None), P(("grp", "pool"), None, None, None)),
            check_vma=False,
        )
        return step(queries, new_kv, pool_kv, hits, blocks, owners)

    return whole
```

```python
import functools
import math

import jax
import jax.numpy as jnp
from jax import lax
from jax.experimental import pallas as pl
from jax.experimental.pallas import tpu as pltpu
from jax.sharding import PartitionSpec as P

MINUS_BIG = -1e30
CHUNK = 8
HBM = pl.BlockSpec(memory_space=pltpu.HBM)
VMEM = pl.BlockSpec(memory_space=pltpu.VMEM)
SMEM = pl.BlockSpec(memory_space=pltpu.SMEM)
GRANT = pltpu.CompilerParams(vmem_limit_bytes=16 << 20)


def owner_position(hits_ref, request, owner, slots, pool):
    first = hits_ref[request, 0] // slots
    return lax.rem(owner - first + pool, pool)


def held_slot(hits_ref, blocks_ref, request, me, slots, pool):
    position = owner_position(hits_ref, request, me, slots, pool)
    longest = hits_ref.shape[1]
    entry = hits_ref[request, jnp.minimum(position, longest - 1)]
    return jnp.where(position < blocks_ref[request], lax.rem(entry, slots), 0)


def wanted_request(owners_ref, device):
    found = jnp.int32(0)
    any_found = jnp.bool_(False)
    for request in range(owners_ref.shape[0]):
        for copy in range(owners_ref.shape[1]):
            hit = owners_ref[request, copy] == device
            found = jnp.where(hit, request, found)
            any_found = jnp.logical_or(any_found, hit)
    return found, any_found


def pack_kernel(plan, sizes, hits_ref, blocks_ref, pool_ref, new_ref, *rest):
    slots, heads, pool = sizes
    outs, (sems,) = rest[: len(plan)], rest[len(plan) :]
    me = lax.axis_index("pool")
    loads = []
    for index, targets in enumerate(plan):
        for place, k in enumerate(targets):
            if k is None:
                source = new_ref.at[0]
            else:
                other = lax.bitwise_xor(me, k)
                slot = held_slot(hits_ref, blocks_ref, other // heads, me, slots, pool)
                source = pool_ref.at[slot, lax.rem(other, heads)]
            load = pltpu.make_async_copy(source, outs[index].at[place], sems.at[len(loads)])
            load.start()
            loads.append(load)
    for load in loads:
        load.wait()


def pack(plan, hits, blocks, pool_kv, new_kv, pool):
    slots, heads, length, width = pool_kv.shape
    rows = sum(len(targets) for targets in plan)
    return pl.pallas_call(
        functools.partial(pack_kernel, plan, (slots, heads, pool)),
        out_shape=[
            jax.ShapeDtypeStruct((len(targets), length, width), pool_kv.dtype) for targets in plan
        ],
        in_specs=[SMEM, SMEM, HBM, HBM],
        out_specs=[VMEM] * len(plan),
        scratch_shapes=[pltpu.SemaphoreType.DMA((rows,))],
        compiler_params=GRANT,
        name="pack",
    )(hits, blocks, pool_kv, new_kv)


def pick(refs, which, store):
    for m, (ref, place) in enumerate(refs):
        @pl.when(which == m)
        def _(ref=ref, place=place):
            store(ref[place])


def route_kernel(late, sizes, owners_ref, cached_ref, *rest):
    heads, requests = sizes
    mine_refs = [(ref, 0) for ref in rest[:requests]]
    over_refs = [(rest[requests], 1)] + [(ref, 0) for ref in rest[requests + 1 : 2 * requests]]
    outs = rest[2 * requests :]
    me = lax.axis_index("pool")
    for index, k in enumerate(late):
        wanted, _ = wanted_request(owners_ref, lax.bitwise_xor(me, k))
        which = lax.bitwise_xor(wanted, me // heads)
        outs[index][0] = cached_ref[index]

        def store_mine(value, index=index):
            outs[index][1] = value

        def store_over(value, index=index):
            outs[index][2] = value

        pick(mine_refs, which, store_mine)
        pick(over_refs, which, store_over)


def route(late, owners, cached, mine, over, heads):
    _, length, width = cached.shape
    return pl.pallas_call(
        functools.partial(route_kernel, late, (heads, len(mine))),
        out_shape=[jax.ShapeDtypeStruct((3, length, width), cached.dtype)] * len(late),
        in_specs=[SMEM] + [VMEM] * (1 + len(mine) + len(over)),
        out_specs=[VMEM] * len(late),
        compiler_params=GRANT,
        name="route",
    )(owners, cached, *mine, *over)


def store_kernel(late, half, sizes, owners_ref, *rest):
    heads, requests = sizes
    mine_refs = [(ref, 0) for ref in rest[:requests]]
    over_refs = [(rest[requests], 1)] + [(ref, 0) for ref in rest[requests + 1 : 2 * requests]]
    pieces, out_ref = rest[2 * requests : -1], rest[-1]
    me = lax.axis_index("pool")
    head = lax.rem(me, heads)
    wanted, owned = wanted_request(owners_ref, me)
    which = lax.bitwise_xor(wanted, me // heads)

    @pl.when(owned)
    def _():
        def store_mine(value):
            out_ref[0, head] = value

        def store_over(value):
            out_ref[0, lax.bitwise_xor(head, half)] = value

        pick(mine_refs, which, store_mine)
        pick(over_refs, which, store_over)
        for piece, k in zip(pieces, late):
            out_ref[0, lax.bitwise_xor(head, k)] = piece[1]
            out_ref[0, lax.bitwise_xor(head, k ^ half)] = piece[2]

    @pl.when(jnp.logical_not(owned))
    def _():
        out_ref[...] = jnp.zeros_like(out_ref)


def store(late, half, owners, mine, over, pieces, heads):
    _, length, width = mine[0].shape
    return pl.pallas_call(
        functools.partial(store_kernel, late, half, (heads, len(mine))),
        out_shape=jax.ShapeDtypeStruct((1, heads, length, width), mine[0].dtype),
        in_specs=[SMEM] + [VMEM] * (len(mine) + len(over) + len(pieces)),
        out_specs=VMEM,
        compiler_params=GRANT,
        name="store",
    )(owners, *mine, *over, *pieces)


def attend_kernel(keys, sizes, first, last, hits_ref, blocks_ref, query_ref, *rest):
    slots, heads, pool, arrays = sizes
    kv_refs, rest = rest[:arrays], rest[arrays:]
    if not first:
        (acc_in, stat_in), rest = rest[:2], rest[2:]
    if last:
        (out_ref,), rest = rest[:1], rest[1:]
    else:
        (acc_out, stat_out), rest = rest[:2], rest[2:]
    (values_ref,) = rest
    me = lax.axis_index("pool")
    request = me // heads
    length = query_ref.shape[1]
    head_dim = values_ref.shape[0]
    groups = query_ref.shape[2] // head_dim
    step = 2 if groups % 2 == 0 else 1
    columns = step * length
    to_exponent = math.log2(math.e) / math.sqrt(head_dim)
    alive = []
    for index, (k, array, place) in enumerate(keys):
        values = kv_refs[array][place, :, head_dim:]
        values_ref[:, index * length : (index + 1) * length] = values.T
        if k is None:
            key_at = lax.broadcasted_iota(jnp.int32, (length, columns), 0)
            token_at = lax.rem(lax.broadcasted_iota(jnp.int32, (length, columns), 1), length)
            alive.append(key_at <= token_at)
        else:
            position = owner_position(hits_ref, request, lax.bitwise_xor(me, k), slots, pool)
            alive.append(position < blocks_ref[request])
    for group in range(0, groups, step):
        at = slice(group * length, (group + step) * length)
        query = jnp.concatenate(
            [query_ref[0, :, h * head_dim : (h + 1) * head_dim] for h in range(group, group + step)],
            0,
        )
        parts = []
        for live, (_k, array, place) in zip(alive, keys):
            scores = lax.dot_general(
                kv_refs[array][place, :, :head_dim],
                query,
                (((1,), (1,)), ((), ())),
                preferred_element_type=jnp.float32,
            )
            parts.append(jnp.where(live, scores, MINUS_BIG))
        top = jnp.max(functools.reduce(jnp.maximum, parts), axis=0, keepdims=True)
        if not first:
            old_top = stat_in[0:1, at]
            top = jnp.maximum(top, old_top)
            factor = jnp.exp2((old_top - top) * to_exponent)
        weights = [jnp.exp2((part - top) * to_exponent) for part in parts]
        total = jnp.sum(functools.reduce(jnp.add, weights), axis=0, keepdims=True)
        mixed = jnp.dot(
            values_ref[...],
            jnp.concatenate([part.astype(jnp.bfloat16) for part in weights], 0),
            preferred_element_type=jnp.float32,
        )
        if not first:
            total = total + stat_in[1:2, at] * factor
            mixed = mixed + acc_in[:, at] * factor
        if last:
            mixed = mixed * (1.0 / total)
            for place, h in enumerate(range(group, group + step)):
                out_ref[0, :, h * head_dim : (h + 1) * head_dim] = mixed[
                    :, place * length : (place + 1) * length
                ].T.astype(out_ref.dtype)
        else:
            acc_out[:, at] = mixed
            stat_out[0:1, at] = top
            stat_out[1:2, at] = total


def attend(keys, hits, blocks, queries, arrays, state, last, slots, heads, pool):
    _, length, columns = queries.shape
    width = arrays[0].shape[-1]
    head_dim = width // 2
    rows = columns // head_dim * length
    first = state is None
    scores = rows * len(keys) * length
    return pl.pallas_call(
        functools.partial(attend_kernel, keys, (slots, heads, pool, len(arrays)), first, last),
        out_shape=jax.ShapeDtypeStruct(queries.shape, queries.dtype)
        if last
        else (
            jax.ShapeDtypeStruct((head_dim, rows), jnp.float32),
            jax.ShapeDtypeStruct((8, rows), jnp.float32),
        ),
        in_specs=[SMEM, SMEM] + [VMEM] * (1 + len(arrays) + (0 if first else 2)),
        out_specs=VMEM if last else (VMEM, VMEM),
        scratch_shapes=[pltpu.VMEM((head_dim, len(keys) * length), jnp.bfloat16)],
        cost_estimate=pl.CostEstimate(
            flops=4 * scores * head_dim,
            bytes_accessed=4 * rows * width,
            transcendentals=scores,
        ),
        compiler_params=GRANT,
    )(hits, blocks, queries, *arrays, *(() if first else state))


def layout(pool, heads):
    far = list(range(heads, pool, 2))
    far = far[len(far) // 2 :] + far[: len(far) // 2]
    half = heads // 2
    return far[:-1], [far[-1], far[-1] ^ 1], list(range(half, heads)), list(range(1, half))


def on_device(pool, queries, new_kv, pool_kv, hits, blocks, owners):
    slots, heads, _, _ = pool_kv.shape
    requests = hits.shape[0]
    far_pairs, far_last, early, late = layout(pool, heads)
    half = heads // 2

    def swap(k, array):
        return lax.ppermute(array, "pool", [(p, p ^ k) for p in range(pool)])

    mine = [new_kv] + [swap(m * heads, new_kv) for m in range(1, requests)]
    plan = [(k, k ^ 1) for k in far_pairs] + [(k,) for k in far_last]
    plan += [(k, None) if k == half else (k,) for k in early] + [(0,), tuple(late)]
    packed = pack(plan, hits, blocks, pool_kv, new_kv, pool)
    own, cached = packed[-2:]
    moved = {}
    for targets, array in zip(plan[:-2], packed):
        moved[targets[0]] = swap(targets[0], array)
    over = [moved[half]] + [swap(half, mine[m]) for m in range(1, requests)]
    routed = route(late, owners, cached, mine, over, heads)
    for k, array in zip(late, routed):
        moved[k] = swap(k, array)
    mates = {k: swap(1, moved[k]) for k in far_pairs}

    near = [(None, new_kv, 0), (0, own, 0)] + [(k, moved[k], 0) for k in early]
    rest = [(k, moved[k], 0) for k in late]
    for k in far_pairs:
        rest += [(k, moved[k], 0), (k ^ 1, mates[k], 1)]
    chunks = [near] + [rest[i : i + CHUNK] for i in range(0, len(rest), CHUNK)]
    chunks += [[(k, moved[k], 0) for k in far_last]]
    state = None
    for number, chunk in enumerate(chunks):
        state = attend(
            [(k, i, place) for i, (k, _, place) in enumerate(chunk)],
            hits, blocks, queries, [array for _, array, _ in chunk], state,
            number == len(chunks) - 1, slots, heads, pool,
        )
    new_store = store(late, half, owners, mine, over, [moved[k] for k in late], heads)
    return state, new_store


def solution(mesh):
    pool = mesh.shape["pool"]
    placed = (
        P(("grp", "pool"), None, None),
        P(("grp", "pool"), None, None),
        P(("grp", "pool"), None, None, None),
        P("grp", None),
        P("grp"),
        P("grp", None),
    )

    def whole(queries, new_kv, pool_kv, hits, blocks, owners):
        step = jax.shard_map(
            functools.partial(on_device, pool),
            mesh=mesh,
            in_specs=placed,
            out_specs=(P(("grp", "pool"), None, None), P(("grp", "pool"), None, None, None)),
            check_vma=False,
        )
        return step(queries, new_kv, pool_kv, hits, blocks, owners)

    return whole
```
